256 devices in a mesh: seq: 64 (over y, x, z_hi, core), fsdp: 4 (over z_lo).
Axes of the slice: x: 4, y: 4, z: 8 (z_hi: 2, z_lo: 4; z = z_hi * 4 + z_lo), core: 2. Of those that a mesh axis runs over, the one named last changes fastest.
Arguments:
- tokens: bfloat16 [40960, 5120], P('seq', 'fsdp'), may hold values from -24 to 24
- w_local: bfloat16 [5120, 3, 1536], P('seq', None, 'fsdp'), may hold values from -0.078125 to 0.078125
- w_strided: bfloat16 [5120, 3, 1024], P('seq', None, 'fsdp'), may hold values from -0.078125 to 0.078125
- valid: int32 [64, 640], P('seq'), may hold values 0 or 1
- band_reach: int32 [12], P('fsdp'), may hold values from 1 to 4, as said below
Outputs:
- out_local: bfloat16 [40960, 1536], P('seq', 'fsdp')
- out_strided: bfloat16 [40960, 1024], P('seq', 'fsdp')
The draws below stay inside these ranges and needn't reach their ends.
Inputs may be any that keep to these rules, and one draw needn't show every extreme that they name: Query block b of local head h sees band blocks b - band_reach[h] to b.
All inputs are finite; a program needn't handle non-finite values. No bound on the sum of `valid` on one device may be relied on, other than what follows from the above.
Results may differ from the reference program's by a relative error of at most 0.012.
The reference program's roundings to bfloat16 on the way count: a program that leaves them out, or rounds other values in their place, can miss the bound.
Values may be sent and summed in bfloat16 or wider, within the bound.
No kernel may reach another device: no remote copies, remote signals or barrier semaphores. Data moves between devices by JAX's collectives and lax.ppermute only.
A program may use at most 128 MiB of HBM per device.

```python
import functools
import math
import jax
import jax.numpy as jnp
from jax import lax

D = 5120
HD = 128
LH = 12
SH = 8
BLK = 128
SEC = 640
NBLK = 5
DAYS = 64
TOKENS = 40960


def draw_tokens(key, part):
    first = jax.random.fold_in(jax.random.fold_in(key, 11), 0)
    values = jnp.clip(jax.random.normal(first, (TOKENS, D), jnp.float32), -6.0, 6.0)
    return values.astype(jnp.bfloat16)


def draw_band_reach(key, part):
    first, second, third = jax.random.split(jax.random.fold_in(key, 23), 3)
    reach = jax.random.randint(first, (LH,), 1, NBLK)
    widest = jax.random.randint(second, (), 0, LH)
    narrowest = (widest + jax.random.randint(third, (), 1, LH)) % LH
    heads = jnp.arange(LH)
    reach = jnp.where(heads == widest, NBLK - 1, reach)
    reach = jnp.where(heads == narrowest, 1, reach)
    return reach.astype(jnp.int32)


def set_ends(drawn, rng, smallest, top_value):
    longest = drawn.shape.index(max(drawn.shape))
    spots = []
    for shift in (0, 1):
        where = [jax.random.randint(jax.random.fold_in(rng, axis), (), 0, length) for axis, length in enumerate(drawn.shape)]
        where[longest] = (where[longest] + shift) % drawn.shape[longest]
        spots.append(tuple(where))
    return drawn.at[spots[0]].set(smallest).at[spots[1]].set(top_value)


def levels(own_key, extent, cuts, least, top_value):
    factor_of, own = 1.0, jax.random.fold_in(own_key, 6)
    for axis_at, shards_of in cuts:
        heights = jnp.exp(jax.random.uniform(jax.random.fold_in(own, axis_at), (shards_of,), jnp.float32, least / len(cuts), top_value / len(cuts)))
        factor_of = factor_of * jnp.repeat(heights, extent[axis_at] // shards_of).reshape([-1 if axis == axis_at else 1 for axis in range(len(extent))])
    return factor_of


def bell_draw(rng, extent, width, most, shards=(), dtype=jnp.bfloat16):
    drawn = width * jax.random.normal(rng, extent, jnp.float32)
    if shards:
        drawn = drawn * levels(rng, extent, shards, -0.22, 0.18)
    return jnp.clip(drawn, -most, most).astype(dtype)


def setup_inputs(seed: int = 0) -> dict:
    arg_keys = jax.random.split(jax.random.key(seed), 6)
    tokens = draw_tokens(jax.random.fold_in(arg_keys[5], 71), 0)
    w_local = bell_draw(arg_keys[1], (D, 3, LH * HD), D ** -0.5, 0.078125, ((0, 64), (2, 4)))
    w_strided = bell_draw(arg_keys[2], (D, 3, SH * HD), D ** -0.5, 0.078125, ((0, 64), (2, 4)))
    valid = set_ends((jax.random.randint(arg_keys[3], (DAYS, SEC), 0, 8) < 7).astype(jnp.int32), jax.random.fold_in(arg_keys[3], 1), 0, 1)
    band_reach = draw_band_reach(jax.random.fold_in(arg_keys[5], 71), 0)
    return dict(tokens=tokens, w_local=w_local, w_strided=w_strided, valid=valid, band_reach=band_reach)


def local_day(band_reach, inputs):
    qkv_day, valid_day = inputs
    query = qkv_day[:, 0].astype(jnp.float32)
    keys = qkv_day[:, 1].astype(jnp.float32)
    values = qkv_day[:, 2].astype(jnp.float32)
    scores = jnp.einsum('qhc,khc->hqk', query, keys) / math.sqrt(HD)
    position = jnp.arange(SEC)
    causal = position[None, :] <= position[:, None]
    block = position // BLK
    band = block[None, None, :] >= block[None, :, None] - band_reach[:, None, None]
    seen = (valid_day[None, :] > 0) | (position[None, :] == position[:, None])
    allowed = causal[None] & band & seen[None]
    scores = jnp.where(allowed, scores, -jnp.inf)
    row_max = lax.optimization_barrier(jnp.max(scores, axis=-1, keepdims=True))
    expo = jnp.exp(scores - row_max)
    probs = (expo / lax.optimization_barrier(jnp.sum(expo, axis=-1, keepdims=True))).astype(jnp.bfloat16)
    result = jnp.einsum('hqk,khc->qhc', probs.astype(jnp.float32), values)
    return result.astype(jnp.bfloat16).reshape(SEC, LH * HD)

def reference(tokens, w_local, w_strided, valid, band_reach):
    qkv_local = jnp.dot(tokens, w_local.reshape(D, 3 * LH * HD), preferred_element_type=jnp.float32).astype(jnp.bfloat16)
    qkv_local = qkv_local.reshape(DAYS, SEC, 3, LH, HD)
    out_local = lax.map(functools.partial(local_day, band_reach), (qkv_local, valid)).reshape(TOKENS, LH * HD)
    qkv_strided = jnp.dot(tokens, w_strided.reshape(D, 3 * SH * HD), preferred_element_type=jnp.float32).astype(jnp.bfloat16)
    qkv_strided = qkv_strided.reshape(DAYS, SEC, 3, SH, HD)
    query = qkv_strided[:, :, 0].astype(jnp.float32)
    keys = qkv_strided[:, :, 1].astype(jnp.float32)
    values = qkv_strided[:, :, 2].astype(jnp.float32)
    scores = jnp.einsum('dshc,eshc->shde', query, keys) / math.sqrt(HD)
    day = jnp.arange(DAYS)
    causal = day[None, :] <= day[:, None]
    same = day[None, :] == day[:, None]
    seen = jnp.transpose(valid) > 0
    allowed = causal[None, None] & (seen[:, None, None, :] | same[None, None])
    scores = jnp.where(allowed, scores, -jnp.inf)
    row_max = lax.optimization_barrier(jnp.max(scores, axis=-1, keepdims=True))
    expo = jnp.exp(scores - row_max)
    probs = (expo / lax.optimization_barrier(jnp.sum(expo, axis=-1, keepdims=True))).astype(jnp.bfloat16)
    result = jnp.einsum('shde,eshc->dshc', probs.astype(jnp.float32), values)
    out_strided = result.astype(jnp.bfloat16).reshape(TOKENS, SH * HD)
    return (out_local, out_strided)
```

```python
import functools
import math

import jax
import jax.numpy as jnp
from jax import lax
from jax.experimental import pallas as pl
from jax.experimental.pallas import tpu as pltpu
from jax.sharding import PartitionSpec as P

HD = 128
BLK = 128
NY, NX, NH, NC = 4, 4, 2, 2
CHUNKS = (320, 320)


def seq_pairs(move):
    pairs = []
    for y in range(NY):
        for x in range(NX):
            for h in range(NH):
                for c in range(NC):
                    ty, tx, th, tc = move(y, x, h, c)
                    pairs.append(
                        (((y * NX + x) * NH + h) * NC + c, ((ty * NX + tx) * NH + th) * NC + tc)
                    )
    return pairs


MOVES = {
    "x1": lambda y, x, h, c: (y, x ^ 1, h, c),
    "x3": lambda y, x, h, c: (y, x ^ 3, h, c),
    "y1": lambda y, x, h, c: (y ^ 1, x, h, c),
    "y3": lambda y, x, h, c: (y ^ 3, x, h, c),
    "h": lambda y, x, h, c: (y, x, 1 - h, c),
    "c": lambda y, x, h, c: (y, x, h, 1 - c),
}
FLIPS = {"x1": (0, 1), "x3": (0, 3), "y1": (1, 0), "y3": (3, 0)}
OWN_ORDERS = (("x1", "x3", "y1", "y3"), ("y1", "y3", "x1", "x3"))
OTHER_ORDERS = (("x3", "y1", "y3", "x1"), ("y3", "x1", "x3", "y1"))


def swap(value, kind):
    return lax.ppermute(value, "seq", seq_pairs(MOVES[kind]))


def double_up(value, order):
    value = value[None]
    for kind in order[:-1]:
        value = jnp.concatenate([value, swap(value, kind)], axis=0)
    received = swap(value, order[-1])
    return [value, received]


def place_kernel(orders, place, *refs):
    pieces = refs[:8]
    out, sem = refs[8:]
    y, x, h, c = (place[i] for i in range(4))
    count, _, part, _ = pieces[0].shape
    for group in range(2):
        half = h if group == 0 else 1 - h
        for last in range(2):
            for side in range(2):
                core = c if side == 0 else 1 - c
                ref = pieces[(group * 2 + last) * 2 + side]
                for k in range(count):
                    flip_y, flip_x = 0, 0
                    for bit, kind in enumerate(orders[group]):
                        if (k + last * count) >> bit & 1:
                            flip_y, flip_x = flip_y ^ FLIPS[kind][0], flip_x ^ FLIPS[kind][1]
                    block = (((y ^ flip_y) * NX + (x ^ flip_x)) * NH + half) * NC + core
                    rows = pl.ds(pl.multiple_of(block * part, 16), part)
                    pltpu.make_async_copy(ref.at[k], out.at[:, rows, :], sem).start()
    pltpu.make_async_copy(out, out, sem).wait()


def place_weights(place, own, other, which):
    pieces = []
    for value, order in ((own, OWN_ORDERS[which]), (other, OTHER_ORDERS[which])):
        for piece in double_up(value, order):
            pieces += [piece, swap(piece, "c")]
    part, cols = own.shape[1:]
    total = NY * NX * NH * NC * part
    return pl.pallas_call(
        functools.partial(place_kernel, (OWN_ORDERS[which], OTHER_ORDERS[which])),
        out_shape=jax.ShapeDtypeStruct((3, total, cols), jnp.bfloat16),
        in_specs=[pl.BlockSpec(memory_space=pltpu.SMEM)]
        + [pl.BlockSpec(memory_space=pltpu.HBM)] * 8,
        out_specs=pl.BlockSpec(memory_space=pltpu.VMEM),
        scratch_shapes=[pltpu.SemaphoreType.DMA],
        compiler_params=pltpu.CompilerParams(vmem_limit_bytes=16 * 1024 * 1024),
        cost_estimate=pl.CostEstimate(
            flops=0, bytes_accessed=4 * 3 * total * cols, transcendentals=0
        ),
    )(place, *pieces)


def project_kernel(tokens, weight, out):
    out[0] = jnp.dot(
        tokens[...], weight[0], preferred_element_type=jnp.float32
    ).astype(out.dtype)


def project(tokens, weight):
    rows, total = tokens.shape
    cols = weight.shape[2]
    return pl.pallas_call(
        project_kernel,
        grid=(3,),
        out_shape=jax.ShapeDtypeStruct((3, rows, cols), jnp.bfloat16),
        in_specs=[
            pl.BlockSpec((rows, total), lambda j: (0, 0)),
            pl.BlockSpec((1, total, cols), lambda j: (j, 0, 0)),
        ],
        out_specs=pl.BlockSpec((1, rows, cols), lambda j: (j, 0, 0)),
        compiler_params=pltpu.CompilerParams(vmem_limit_bytes=40 * 1024 * 1024),
        cost_estimate=pl.CostEstimate(
            flops=2 * rows * total * 3 * cols,
            bytes_accessed=2 * (rows * total + 3 * total * cols + 3 * rows * cols),
            transcendentals=0,
        ),
    )(tokens, weight)


def local_attend(qkv, valid_day, reach):
    query, keys, values = qkv[0], qkv[1], qkv[2]
    seconds = query.shape[0]
    query = query.reshape(seconds, -1, HD)
    keys = keys.reshape(seconds, -1, HD)
    values = values.reshape(seconds, -1, HD)
    scores = jnp.einsum(
        "qhc,khc->hqk", query, keys, preferred_element_type=jnp.float32
    ) / math.sqrt(HD)
    position = jnp.arange(seconds)
    causal = position[None, :] <= position[:, None]
    block = position // BLK
    band = block[None, None, :] >= block[None, :, None] - reach[:, None, None]
    seen = (valid_day[None, :] > 0) | (position[None, :] == position[:, None])
    allowed = causal[None] & band & seen[None]
    scores = jnp.where(allowed, scores, -jnp.inf)
    row_max = jnp.max(scores, axis=-1, keepdims=True)
    expo = jnp.exp(scores - row_max)
    probs = (expo / jnp.sum(expo, axis=-1, keepdims=True)).astype(jnp.bfloat16)
    result = jnp.einsum("hqk,khc->qhc", probs, values, preferred_element_type=jnp.float32)
    return result.astype(jnp.bfloat16).reshape(seconds, -1)


def strided_attend(qkv, marks):
    rows, cols = qkv.shape[1:]
    peers = NY * NX * NH * NC
    count = rows // peers
    heads = cols // HD
    packed = qkv.reshape(3, peers, count, heads, HD).transpose(1, 0, 3, 2, 4)
    packed = packed.reshape(peers, 3 * heads * count, HD)
    flags = marks.astype(jnp.bfloat16).reshape(peers, 1, count)
    flags = jnp.pad(flags, ((0, 0), (0, 0), (0, HD - count)))
    packed = jnp.concatenate([packed, flags], axis=1)
    packed = lax.all_to_all(packed, "seq", split_axis=0, concat_axis=0, tiled=True)
    days = packed.shape[0]
    split_up = packed[:, :-1].reshape(days, 3, heads, count, HD)
    query, keys, values = split_up[:, 0], split_up[:, 1], split_up[:, 2]
    scores = jnp.einsum(
        "dhsc,ehsc->hsde", query, keys, preferred_element_type=jnp.float32
    ) / math.sqrt(HD)
    day = jnp.arange(days)
    causal = day[None, :] <= day[:, None]
    same = day[None, :] == day[:, None]
    seen = jnp.transpose(packed[:, -1, :count]) > 0
    allowed = causal[None] & (seen[:, None, :] | same[None])
    scores = jnp.where(allowed[None], scores, -jnp.inf)
    row_max = jnp.max(scores, axis=-1, keepdims=True)
    expo = jnp.exp(scores - row_max)
    probs = (expo / jnp.sum(expo, axis=-1, keepdims=True)).astype(jnp.bfloat16)
    result = jnp.einsum("hsde,ehsc->dhsc", probs, values, preferred_element_type=jnp.float32)
    result = result.astype(jnp.bfloat16).reshape(days, heads * count, HD)
    result = lax.all_to_all(result, "seq", split_axis=0, concat_axis=0, tiled=True)
    result = result.reshape(peers, heads, count, HD).transpose(0, 2, 1, 3)
    return result.reshape(rows, cols)


def body(tokens, w_local, w_strided, valid, band_reach):
    seq = lax.axis_index("seq")
    place = jnp.stack(
        [
            seq // (NX * NH * NC),
            seq // (NH * NC) % NX,
            seq // NC % NH,
            seq % NC,
            lax.axis_index("fsdp"),
        ]
    ).astype(jnp.int32)
    own_strided = jnp.transpose(w_strided, (1, 0, 2))
    own_local = jnp.transpose(w_local, (1, 0, 2))
    other_strided = swap(own_strided, "h")
    other_local = swap(own_local, "h")
    tokens, other_strided, other_local = lax.optimization_barrier(
        (tokens, other_strided, other_local)
    )
    weight_strided = place_weights(place, own_strided, other_strided, 0)
    weight_local = place_weights(place, own_local, other_local, 1)
    out_strided, qkv_local = [], []
    start = 0
    for size in CHUNKS:
        rows = slice(start, start + size)
        gathered = lax.all_gather(tokens[rows], "fsdp", axis=1, tiled=True)
        qkv = project(gathered, weight_strided)
        out_strided.append(strided_attend(qkv, valid[0, rows]))
        qkv_local.append(project(gathered, weight_local))
        start += size
    out_strided = jnp.concatenate(out_strided, axis=0)
    qkv_local = jnp.concatenate(qkv_local, axis=1)
    out_local = local_attend(qkv_local, valid[0], band_reach)
    return (out_local, out_strided)


def solution(mesh):
    in_specs = (
        P("seq", "fsdp"),
        P("seq", None, "fsdp"),
        P("seq", None, "fsdp"),
        P("seq", None),
        P("fsdp"),
    )
    out_specs = (P("seq", "fsdp"), P("seq", "fsdp"))
    return jax.shard_map(body, mesh=mesh, in_specs=in_specs, out_specs=out_specs, check_vma=False)
```

```python
import functools
import math

import jax
import jax.numpy as jnp
from jax import lax
from jax.experimental import pallas as pl
from jax.experimental.pallas import tpu as pltpu
from jax.sharding import PartitionSpec as P

HD = 128
BLK = 128
NY, NX, NH, NC = 4, 4, 2, 2
NZ = 4


def seq_pairs(move):
    pairs = []
    for y in range(NY):
        for x in range(NX):
            for h in range(NH):
                for c in range(NC):
                    ty, tx, th, tc = move(y, x, h, c)
                    pairs.append(
                        (((y * NX + x) * NH + h) * NC + c, ((ty * NX + tx) * NH + th) * NC + tc)
                    )
    return pairs


MOVES = {
    "x1": lambda y, x, h, c: (y, x ^ 1, h, c),
    "x3": lambda y, x, h, c: (y, x ^ 3, h, c),
    "y1": lambda y, x, h, c: (y ^ 1, x, h, c),
    "y3": lambda y, x, h, c: (y ^ 3, x, h, c),
    "h": lambda y, x, h, c: (y, x, 1 - h, c),
    "c": lambda y, x, h, c: (y, x, h, 1 - c),
}
FLIPS = {"x1": (0, 1), "x3": (0, 3), "y1": (1, 0), "y3": (3, 0)}
OWN_ORDERS = (("x1", "x3", "y1", "y3"), ("y1", "y3", "x1", "x3"))
OTHER_ORDERS = (("x3", "y1", "y3", "x1"), ("y3", "x1", "x3", "y1"))


def swap(value, kind):
    return lax.ppermute(value, "seq", seq_pairs(MOVES[kind]))


def double_up(value, order):
    value = value[None]
    for kind in order[:-1]:
        value = jnp.concatenate([value, swap(value, kind)], axis=0)
    received = swap(value, order[-1])
    return [value, received]


def place_kernel(orders, place, *refs):
    pieces = refs[:8]
    out, sem = refs[8:]
    y, x, h, c = (place[i] for i in range(4))
    count, _, part, _ = pieces[0].shape
    for group in range(2):
        half = h if group == 0 else 1 - h
        for last in range(2):
            for side in range(2):
                core = c if side == 0 else 1 - c
                ref = pieces[(group * 2 + last) * 2 + side]
                for k in range(count):
                    flip_y, flip_x = 0, 0
                    for bit, kind in enumerate(orders[group]):
                        if (k + last * count) >> bit & 1:
                            flip_y, flip_x = flip_y ^ FLIPS[kind][0], flip_x ^ FLIPS[kind][1]
                    block = (((y ^ flip_y) * NX + (x ^ flip_x)) * NH + half) * NC + core
                    rows = pl.ds(pl.multiple_of(block * part, 16), part)
                    pltpu.make_async_copy(ref.at[k], out.at[:, rows, :], sem).start()
    pltpu.make_async_copy(out, out, sem).wait()


def place_weights(place, own, other, which):
    pieces = []
    for value, order in ((own, OWN_ORDERS[which]), (other, OTHER_ORDERS[which])):
        for piece in double_up(value, order):
            pieces += [piece, swap(piece, "c")]
    part, cols = own.shape[1:]
    total = NY * NX * NH * NC * part
    return pl.pallas_call(
        functools.partial(place_kernel, (OWN_ORDERS[which], OTHER_ORDERS[which])),
        out_shape=jax.ShapeDtypeStruct((3, total, cols), jnp.bfloat16),
        in_specs=[pl.BlockSpec(memory_space=pltpu.SMEM)]
        + [pl.BlockSpec(memory_space=pltpu.HBM)] * 8,
        out_specs=pl.BlockSpec(memory_space=pltpu.VMEM),
        scratch_shapes=[pltpu.SemaphoreType.DMA],
        compiler_params=pltpu.CompilerParams(vmem_limit_bytes=16 * 1024 * 1024),
        cost_estimate=pl.CostEstimate(
            flops=0, bytes_accessed=4 * 3 * total * cols, transcendentals=0
        ),
    )(place, *[pltpu.with_memory_space_constraint(piece, pltpu.HBM) for piece in pieces])


def project_kernel(tokens, weight, out, held, sem, *loaded):
    depth = held.shape[1] // NZ

    def copy(k):
        cols = pl.ds(k * depth, depth)
        return pltpu.make_async_copy(tokens.at[:, cols], held.at[:, cols], sem.at[k])

    def load(j, k):
        rows = pl.ds(k * depth, depth)
        return pltpu.make_async_copy(
            weight.at[j, rows, :], loaded[0].at[j, rows, :], loaded[1].at[j, k]
        )

    factor = loaded[0] if loaded else weight
    for k in range(NZ):
        copy(k).start()
        if loaded:
            load(0, k).start()
    if loaded:
        for j in range(1, 3):
            for k in range(NZ):
                load(j, k).start()
    acc = None
    for k in range(NZ):
        copy(k).wait()
        if loaded:
            load(0, k).wait()
        cols = slice(k * depth, (k + 1) * depth)
        term = jnp.dot(held[:, cols], factor[0, cols], preferred_element_type=jnp.float32)
        acc = term if acc is None else acc + term
    out[0] = acc.astype(out.dtype)

    def step(j, carry):
        if loaded:
            for k in range(NZ):
                load(j, k).wait()
        out[j] = jnp.dot(
            held[...], factor[j], preferred_element_type=jnp.float32
        ).astype(out.dtype)
        return carry

    lax.fori_loop(1, 3, step, 0)


def project(tokens, weight, load):
    rows, total = tokens.shape
    cols = weight.shape[2]
    scratch = [pltpu.VMEM((rows, total), jnp.bfloat16), pltpu.SemaphoreType.DMA((NZ,))]
    if load:
        weight = pltpu.with_memory_space_constraint(weight, pltpu.HBM)
        scratch += [
            pltpu.VMEM((3, total, cols), jnp.bfloat16),
            pltpu.SemaphoreType.DMA((3, NZ)),
        ]
    return pl.pallas_call(
        project_kernel,
        out_shape=jax.ShapeDtypeStruct((3, rows, cols), jnp.bfloat16),
        in_specs=[
            pl.BlockSpec(memory_space=pltpu.HBM),
            pl.BlockSpec(memory_space=pltpu.HBM if load else pltpu.VMEM),
        ],
        out_specs=pl.BlockSpec(memory_space=pltpu.VMEM),
        scratch_shapes=scratch,
        compiler_params=pltpu.CompilerParams(vmem_limit_bytes=20 * 1024 * 1024),
        cost_estimate=pl.CostEstimate(
            flops=2 * rows * total * 3 * cols,
            bytes_accessed=2 * (rows * total + 3 * total * cols + 3 * rows * cols),
            transcendentals=0,
        ),
    )(pltpu.with_memory_space_constraint(tokens, pltpu.HBM), weight)


def local_attend(qkv, valid_day, reach):
    query, keys, values = qkv[0], qkv[1], qkv[2]
    seconds = query.shape[0]
    query = query.reshape(seconds, -1, HD)
    keys = keys.reshape(seconds, -1, HD)
    values = values.reshape(seconds, -1, HD)
    scores = jnp.einsum(
        "qhc,khc->hqk", query, keys, preferred_element_type=jnp.float32
    ) / math.sqrt(HD)
    position = jnp.arange(seconds)
    causal = position[None, :] <= position[:, None]
    block = position // BLK
    band = block[None, None, :] >= block[None, :, None] - reach[:, None, None]
    seen = (valid_day[None, :] > 0) | (position[None, :] == position[:, None])
    allowed = causal[None] & band & seen[None]
    scores = jnp.where(allowed, scores, -jnp.inf)
    row_max = jnp.max(scores, axis=-1, keepdims=True)
    expo = jnp.exp(scores - row_max)
    probs = (expo / jnp.sum(expo, axis=-1, keepdims=True)).astype(jnp.bfloat16)
    result = jnp.einsum("hqk,khc->qhc", probs, values, preferred_element_type=jnp.float32)
    return result.astype(jnp.bfloat16).reshape(seconds, -1)


def strided_attend(qkv, marks):
    rows, cols = qkv.shape[1:]
    peers = NY * NX * NH * NC
    count = rows // peers
    heads = cols // HD
    packed = qkv.reshape(3, peers, count, heads, HD).transpose(1, 0, 3, 2, 4)
    packed = packed.reshape(peers, 3 * heads * count, HD)
    flags = marks.astype(jnp.bfloat16).reshape(peers, 1, count)
    flags = jnp.pad(flags, ((0, 0), (0, 0), (0, HD - count)))
    packed = jnp.concatenate([packed, flags], axis=1)
    packed = lax.all_to_all(packed, "seq", split_axis=0, concat_axis=0, tiled=True)
    days = packed.shape[0]
    split_up = packed[:, :-1].reshape(days, 3, heads, count, HD)
    query, keys, values = split_up[:, 0], split_up[:, 1], split_up[:, 2]
    scores = jnp.einsum(
        "dhsc,ehsc->hsde", query, keys, preferred_element_type=jnp.float32
    ) / math.sqrt(HD)
    day = jnp.arange(days)
    causal = day[None, :] <= day[:, None]
    same = day[None, :] == day[:, None]
    seen = jnp.transpose(packed[:, -1, :count]) > 0
    allowed = causal[None] & (seen[:, None, :] | same[None])
    scores = jnp.where(allowed[None], scores, -jnp.inf)
    row_max = jnp.max(scores, axis=-1, keepdims=True)
    expo = jnp.exp(scores - row_max)
    probs = (expo / jnp.sum(expo, axis=-1, keepdims=True)).astype(jnp.bfloat16)
    result = jnp.einsum("hsde,ehsc->dhsc", probs, values, preferred_element_type=jnp.float32)
    result = result.astype(jnp.bfloat16).reshape(days, heads * count, HD)
    result = lax.all_to_all(result, "seq", split_axis=0, concat_axis=0, tiled=True)
    result = result.reshape(peers, heads, count, HD).transpose(0, 2, 1, 3)
    return result.reshape(rows, cols)


def body(tokens, w_local, w_strided, valid, band_reach):
    seq = lax.axis_index("seq")
    place = jnp.stack(
        [
            seq // (NX * NH * NC),
            seq // (NH * NC) % NX,
            seq // NC % NH,
            seq % NC,
            lax.axis_index("fsdp"),
        ]
    ).astype(jnp.int32)
    own_strided = jnp.transpose(w_strided, (1, 0, 2))
    own_local = jnp.transpose(w_local, (1, 0, 2))
    other_strided = swap(own_strided, "h")
    other_local = swap(own_local, "h")
    weight_strided = place_weights(place, own_strided, other_strided, 0)
    weight_local = place_weights(place, own_local, other_local, 1)
    gathered = lax.all_gather(tokens, "fsdp", axis=1, tiled=True)
    out_strided = strided_attend(project(gathered, weight_strided, True), valid[0])
    qkv_local = project(gathered, weight_local, False)
    out_local = local_attend(qkv_local, valid[0], band_reach)
    return (out_local, out_strided)


def solution(mesh):
    in_specs = (
        P("seq", "fsdp"),
        P("seq", None, "fsdp"),
        P("seq", None, "fsdp"),
        P("seq", None),
        P("fsdp"),
    )
    out_specs = (P("seq", "fsdp"), P("seq", "fsdp"))
    return jax.shard_map(body, mesh=mesh, in_specs=in_specs, out_specs=out_specs, check_vma=False)
```

```python
import functools
import math

import jax
import jax.numpy as jnp
from jax import lax
from jax.experimental import pallas as pl
from jax.experimental.pallas import tpu as pltpu
from jax.sharding import PartitionSpec as P

HD = 128
BLK = 128
NY, NX, NH, NC = 4, 4, 2, 2
NZ = 4


def seq_pairs(move):
    pairs = []
    for y in range(NY):
        for x in range(NX):
            for h in range(NH):
                for c in range(NC):
                    ty, tx, th, tc = move(y, x, h, c)
                    pairs.append(
                        (((y * NX + x) * NH + h) * NC + c, ((ty * NX + tx) * NH + th) * NC + tc)
                    )
    return pairs


MOVES = {
    "x1": lambda y, x, h, c: (y, x ^ 1, h, c),
    "x3": lambda y, x, h, c: (y, x ^ 3, h, c),
    "y1": lambda y, x, h, c: (y ^ 1, x, h, c),
    "y3": lambda y, x, h, c: (y ^ 3, x, h, c),
    "h": lambda y, x, h, c: (y, x, 1 - h, c),
    "c": lambda y, x, h, c: (y, x, h, 1 - c),
}
FLIPS = {"x1": (0, 1), "x3": (0, 3), "y1": (1, 0), "y3": (3, 0)}
OWN_ORDERS = (("x1", "x3", "y1", "y3"), ("x1", "x3", "y3", "y1"))
OTHER_ORDERS = (("y1", "y3", "x1", "x3"), ("y1", "y3", "x3", "x1"))


def swap(value, kind):
    return lax.ppermute(value, "seq", seq_pairs(MOVES[kind]))


def advance(value, kind):
    return jnp.concatenate([value, swap(value, kind)], axis=0)


def place_kernel(orders, place, *refs):
    pieces = refs[:8]
    out, sem = refs[8:]
    y, x, h, c = (place[i] for i in range(4))
    count, _, part, _ = pieces[0].shape
    for group in range(2):
        half = h if group == 0 else 1 - h
        for last in range(2):
            for side in range(2):
                core = c if side == 0 else 1 - c
                ref = pieces[(group * 2 + last) * 2 + side]
                for k in range(count):
                    flip_y, flip_x = 0, 0
                    for bit, kind in enumerate(orders[group]):
                        if (k + last * count) >> bit & 1:
                            flip_y, flip_x = flip_y ^ FLIPS[kind][0], flip_x ^ FLIPS[kind][1]
                    block = (((y ^ flip_y) * NX + (x ^ flip_x)) * NH + half) * NC + core
                    rows = pl.ds(pl.multiple_of(block * part, 16), part)
                    pltpu.make_async_copy(ref.at[k], out.at[:, rows, :], sem).start()
    pltpu.make_async_copy(out, out, sem).wait()


def place_weights(place, held, received, which):
    held_swapped = [swap(piece, "c") for piece in held]
    received_swapped = [swap(piece, "c") for piece in received]
    pieces = []
    for group in range(2):
        pieces += [held[group], held_swapped[group]]
        pieces += [received[group], received_swapped[group]]
    part, cols = pieces[0].shape[2:]
    total = NY * NX * NH * NC * part
    return pl.pallas_call(
        functools.partial(place_kernel, (OWN_ORDERS[which], OTHER_ORDERS[which])),
        out_shape=jax.ShapeDtypeStruct((3, total, cols), jnp.bfloat16),
        in_specs=[pl.BlockSpec(memory_space=pltpu.SMEM)]
        + [pl.BlockSpec(memory_space=pltpu.HBM)] * 8,
        out_specs=pl.BlockSpec(memory_space=pltpu.VMEM),
        scratch_shapes=[pltpu.SemaphoreType.DMA],
        compiler_params=pltpu.CompilerParams(vmem_limit_bytes=16 * 1024 * 1024),
        cost_estimate=pl.CostEstimate(
            flops=0, bytes_accessed=4 * 3 * total * cols, transcendentals=0
        ),
    )(place, *[pltpu.with_memory_space_constraint(piece, pltpu.HBM) for piece in pieces])


def send_z(value, pairs):
    return lax.ppermute(value, "fsdp", pairs)


def advance_both(pair, which, step):
    return [
        advance(value, orders[which][step])
        for value, orders in zip(pair, (OWN_ORDERS, OTHER_ORDERS))
    ]


def finish_both(pair, which):
    return [
        swap(value, orders[which][3]) for value, orders in zip(pair, (OWN_ORDERS, OTHER_ORDERS))
    ]


def gather_all(tokens, own_strided, own_local):
    split = own_strided.shape[2]
    own = jnp.concatenate([own_strided, own_local], axis=2)[None]
    other = swap(own, "h")
    tokens, other = lax.optimization_barrier((tokens, other))
    near = send_z(tokens, [(0, 1), (1, 0), (2, 3), (3, 2)])
    middle = send_z(tokens, [(1, 2), (2, 1)])
    pair = [own, other]
    for step in range(2):
        pair = advance_both(pair, 0, step)
    strided = advance_both([value[..., :split] for value in pair], 0, 2)
    local = [value[..., split:] for value in pair]
    near, middle, strided, local = lax.optimization_barrier((near, middle, strided, local))
    across = send_z(near, [(1, 2), (2, 1)])
    outward = send_z(middle, [(2, 3), (1, 0)])
    local = advance_both(local, 1, 2)
    received = finish_both(strided, 0)
    across, outward, received, local = lax.optimization_barrier(
        (across, outward, received, local)
    )
    far = send_z(across, [(2, 3), (1, 0)])
    received_local = finish_both(local, 1)
    gathered = (tokens, near, middle, across, outward, far)
    return gathered, (strided, received), (local, received_local)


def shard_slots(z, f):
    if f == z:
        return 0
    if abs(f - z) == 3:
        return 5
    if abs(f - z) == 2:
        return 3 if z in (1, 2) else 4
    return 2 if {f, z} == {1, 2} else 1


def for_shard(z, f, slots, action):
    for slot in slots:
        planes = [plane for plane in range(NZ) if shard_slots(plane, f) == slot]
        if planes:
            here = z == planes[0]
            for plane in planes[1:]:
                here = here | (z == plane)

            @pl.when(here)
            def _(slot=slot):
                action(slot)


def early_kernel(place, *refs):
    tokens, weight = refs[:5], refs[5]
    acc, held, factor, token_sem, weight_sem = refs[6:]
    z = place[4]
    depth = held.shape[2]

    def load(f):
        rows = pl.ds(pl.multiple_of(f * depth, depth), depth)
        return pltpu.make_async_copy(
            weight.at[:, rows, :], factor.at[:, rows, :], weight_sem.at[f]
        )

    for f in range(NZ):
        load(f).start()
        for_shard(
            z,
            f,
            range(5),
            lambda slot, f=f: pltpu.make_async_copy(
                tokens[slot], held.at[f], token_sem.at[f]
            ).start(),
        )
    acc[...] = jnp.zeros_like(acc)

    def step(f, carry):
        load(f).wait()

        @pl.when(jnp.abs(f - z) < NZ - 1)
        def _():
            pltpu.make_async_copy(tokens[0], held.at[f], token_sem.at[f]).wait()
            rows = pl.ds(pl.multiple_of(f * depth, depth), depth)
            for j in range(3):
                acc[j] += jnp.dot(
                    held[f], factor[j, rows, :], preferred_element_type=jnp.float32
                )

        return carry

    lax.fori_loop(0, NZ, step, 0)


def late_kernel(place, far, weight, acc, out, held, factor, token_sem, weight_sem):
    z = place[4]
    depth = held.shape[1]
    last = (z == 0) | (z == NZ - 1)
    start = pl.multiple_of(jnp.where(z == 0, (NZ - 1) * depth, 0), depth)

    def load(j):
        return pltpu.make_async_copy(
            weight.at[j, pl.ds(start, depth), :], factor.at[j], weight_sem.at[j]
        )

    @pl.when(last)
    def _():
        pltpu.make_async_copy(far, held, token_sem).start()
        for j in range(3):
            load(j).start()
        pltpu.make_async_copy(far, held, token_sem).wait()

        def step(j, carry):
            load(j).wait()
            term = jnp.dot(held[...], factor[j], preferred_element_type=jnp.float32)
            out[j] = (acc[j] + term).astype(out.dtype)
            return carry

        lax.fori_loop(0, 3, step, 0)

    @pl.when(jnp.logical_not(last))
    def _():
        out[...] = acc[...].astype(out.dtype)


HBM = pl.BlockSpec(memory_space=pltpu.HBM)
VMEM = pl.BlockSpec(memory_space=pltpu.VMEM)
SMEM = pl.BlockSpec(memory_space=pltpu.SMEM)


def in_hbm(values):
    return [pltpu.with_memory_space_constraint(value, pltpu.HBM) for value in values]


def project_early(place, gathered, weight):
    rows, depth = gathered[0].shape
    _, total, cols = weight.shape
    return pl.pallas_call(
        early_kernel,
        out_shape=jax.ShapeDtypeStruct((3, rows, cols), jnp.float32),
        in_specs=[SMEM] + [HBM] * 6,
        out_specs=VMEM,
        scratch_shapes=[
            pltpu.VMEM((NZ, rows, depth), jnp.bfloat16),
            pltpu.VMEM((3, total, cols), jnp.bfloat16),
            pltpu.SemaphoreType.DMA((NZ,)),
            pltpu.SemaphoreType.DMA((NZ,)),
        ],
        compiler_params=pltpu.CompilerParams(vmem_limit_bytes=24 * 1024 * 1024),
        cost_estimate=pl.CostEstimate(
            flops=6 * rows * total * cols,
            bytes_accessed=2 * (rows * total + 3 * total * cols) + 12 * rows * cols,
            transcendentals=0,
        ),
    )(place, *in_hbm(gathered[:5] + (weight,)))


def project_late(place, gathered, weight, acc):
    rows, depth = gathered[0].shape
    cols = weight.shape[2]
    return pl.pallas_call(
        late_kernel,
        out_shape=jax.ShapeDtypeStruct((3, rows, cols), jnp.bfloat16),
        in_specs=[SMEM, HBM, HBM, VMEM],
        out_specs=VMEM,
        scratch_shapes=[
            pltpu.VMEM((rows, depth), jnp.bfloat16),
            pltpu.VMEM((3, depth, cols), jnp.bfloat16),
            pltpu.SemaphoreType.DMA,
            pltpu.SemaphoreType.DMA((3,)),
        ],
        compiler_params=pltpu.CompilerParams(vmem_limit_bytes=16 * 1024 * 1024),
        cost_estimate=pl.CostEstimate(
            flops=6 * rows * depth * cols,
            bytes_accessed=2 * (rows * depth + 3 * depth * cols) + 18 * rows * cols,
            transcendentals=0,
        ),
    )(place, *in_hbm((gathered[5], weight)), acc)


def project_kernel(place, *refs):
    tokens, weight = refs[:6], refs[6]
    out, held, sem = refs[7:]
    depth = held.shape[1] // NZ
    for f in range(NZ):
        cols = held.at[:, pl.ds(f * depth, depth)]
        for_shard(
            place[4],
            f,
            range(6),
            lambda slot, f=f, cols=cols: pltpu.make_async_copy(
                tokens[slot], cols, sem.at[f]
            ).start(),
        )
    for f in range(NZ):
        cols = held.at[:, pl.ds(f * depth, depth)]
        pltpu.make_async_copy(tokens[0], cols, sem.at[f]).wait()

    def step(j, carry):
        out[j] = jnp.dot(
            held[...], weight[j], preferred_element_type=jnp.float32
        ).astype(out.dtype)
        return carry

    lax.fori_loop(0, 3, step, 0)


def project_local(place, gathered, weight):
    rows, depth = gathered[0].shape
    _, total, cols = weight.shape
    return pl.pallas_call(
        project_kernel,
        out_shape=jax.ShapeDtypeStruct((3, rows, cols), jnp.bfloat16),
        in_specs=[SMEM] + [HBM] * 6 + [VMEM],
        out_specs=VMEM,
        scratch_shapes=[
            pltpu.VMEM((rows, total), jnp.bfloat16),
            pltpu.SemaphoreType.DMA((NZ,)),
        ],
        compiler_params=pltpu.CompilerParams(vmem_limit_bytes=20 * 1024 * 1024),
        cost_estimate=pl.CostEstimate(
            flops=6 * rows * total * cols,
            bytes_accessed=2 * (rows * total + 3 * total * cols + 3 * rows * cols),
            transcendentals=0,
        ),
    )(place, *in_hbm(gathered), weight)


def local_attend(qkv, valid_day, reach):
    query, keys, values = qkv[0], qkv[1], qkv[2]
    seconds = query.shape[0]
    query = query.reshape(seconds, -1, HD)
    keys = keys.reshape(seconds, -1, HD)
    values = values.reshape(seconds, -1, HD)
    scores = jnp.einsum(
        "qhc,khc->hqk", query, keys, preferred_element_type=jnp.float32
    ) / math.sqrt(HD)
    position = jnp.arange(seconds)
    causal = position[None, :] <= position[:, None]
    block = position // BLK
    band = block[None, None, :] >= block[None, :, None] - reach[:, None, None]
    seen = (valid_day[None, :] > 0) | (position[None, :] == position[:, None])
    allowed = causal[None] & band & seen[None]
    scores = jnp.where(allowed, scores, -jnp.inf)
    row_max = jnp.max(scores, axis=-1, keepdims=True)
    expo = jnp.exp(scores - row_max)
    probs = (expo / jnp.sum(expo, axis=-1, keepdims=True)).astype(jnp.bfloat16)
    result = jnp.einsum("hqk,khc->qhc", probs, values, preferred_element_type=jnp.float32)
    return result.astype(jnp.bfloat16).reshape(seconds, -1)


def strided_kernel(count, heads, packed, out):
    days = packed.shape[1]
    flags = jnp.transpose(packed[3 * heads * count].astype(jnp.float32))
    span = 2 * days
    row = lax.broadcasted_iota(jnp.int32, (span, span), 0)
    col = lax.broadcasted_iota(jnp.int32, (span, span), 1)
    paired = (row // days) == (col // days)
    earlier = paired & (col < row)
    for second in range(0, count, 2):
        seen = jnp.concatenate(
            [flags[second : second + 1, :], flags[second + 1 : second + 2, :]], axis=1
        )
        allowed = (earlier & (seen > 0)) | (row == col)
        for head in range(heads):
            at = head * count + second
            query, keys, values = (
                packed[pl.ds(at + j * heads * count, 2)].reshape(span, HD) for j in range(3)
            )
            scores = lax.dot_general(
                query, keys, (((1,), (1,)), ((), ())), preferred_element_type=jnp.float32
            ) / math.sqrt(HD)
            scores = jnp.where(allowed, scores, -jnp.inf)
            row_max = jnp.max(scores, axis=1, keepdims=True)
            expo = jnp.exp(scores - row_max)
            probs = (expo / jnp.sum(expo, axis=1, keepdims=True)).astype(jnp.bfloat16)
            result = jnp.dot(probs, values, preferred_element_type=jnp.float32)
            out[pl.ds(at, 2)] = result.astype(jnp.bfloat16).reshape(2, days, HD)


def strided_attend(qkv, marks):
    rows, cols = qkv.shape[1:]
    peers = NY * NX * NH * NC
    count = rows // peers
    heads = cols // HD
    packed = qkv.reshape(3, peers, count, heads, HD).transpose(1, 0, 3, 2, 4)
    packed = packed.reshape(peers, 3 * heads * count, HD)
    flags = marks.astype(jnp.bfloat16).reshape(peers, 1, count)
    flags = jnp.pad(flags, ((0, 0), (0, 0), (0, HD - count)))
    packed = jnp.concatenate([packed, flags], axis=1)
    packed = lax.all_to_all(packed, "seq", split_axis=0, concat_axis=0, tiled=True)
    packed = packed.transpose(1, 0, 2)
    result = pl.pallas_call(
        functools.partial(strided_kernel, count, heads),
        out_shape=jax.ShapeDtypeStruct((heads * count, peers, HD), jnp.bfloat16),
        in_specs=[VMEM],
        out_specs=VMEM,
        compiler_params=pltpu.CompilerParams(vmem_limit_bytes=8 * 1024 * 1024),
        cost_estimate=pl.CostEstimate(
            flops=8 * heads * count * peers * peers * HD,
            bytes_accessed=2 * 4 * heads * count * peers * HD,
            transcendentals=2 * heads * count * peers * peers,
        ),
    )(packed)
    result = result.transpose(1, 0, 2)
    result = lax.all_to_all(result, "seq", split_axis=0, concat_axis=0, tiled=True)
    result = result.reshape(peers, heads, count, HD).transpose(0, 2, 1, 3)
    return result.reshape(rows, cols)


def body(tokens, w_local, w_strided, valid, band_reach):
    seq = lax.axis_index("seq")
    place = jnp.stack(
        [
            seq // (NX * NH * NC),
            seq // (NH * NC) % NX,
            seq // NC % NH,
            seq % NC,
            lax.axis_index("fsdp"),
        ]
    ).astype(jnp.int32)
    own_strided = jnp.transpose(w_strided, (1, 0, 2))
    own_local = jnp.transpose(w_local, (1, 0, 2))
    gathered, strided, local = gather_all(tokens, own_strided, own_local)
    weight_strided = place_weights(place, *strided, 0)
    acc = project_early(place, gathered, weight_strided)
    acc, received = lax.optimization_barrier((acc, local[1]))
    weight_local = place_weights(place, local[0], received, 1)
    qkv_strided = project_late(place, gathered, weight_strided, acc)
    out_strided = strided_attend(qkv_strided, valid[0])
    qkv_local = project_local(place, gathered, weight_local)
    out_local = local_attend(qkv_local, valid[0], band_reach)
    return (out_local, out_strided)


def solution(mesh):
    in_specs = (
        P("seq", "fsdp"),
        P("seq", None, "fsdp"),
        P("seq", None, "fsdp"),
        P("seq", None),
        P("fsdp"),
    )
    out_specs = (P("seq", "fsdp"), P("seq", "fsdp"))
    return jax.shard_map(body, mesh=mesh, in_specs=in_specs, out_specs=out_specs, check_vma=False)
```

```python
import functools
import math

import jax
import jax.numpy as jnp
from jax import lax
from jax.experimental import pallas as pl
from jax.experimental.pallas import tpu as pltpu
from jax.sharding import PartitionSpec as P

HD = 128
BLK = 128
NY, NX, NH, NC = 4, 4, 2, 2
NZ = 4


HBM = pl.BlockSpec(memory_space=pltpu.HBM)
VMEM = pl.BlockSpec(memory_space=pltpu.VMEM)
SMEM = pl.BlockSpec(memory_space=pltpu.SMEM)


def in_hbm(values):
    return [pltpu.with_memory_space_constraint(value, pltpu.HBM) for value in values]


def seq_pairs(move):
    pairs = []
    for y in range(NY):
        for x in range(NX):
            for h in range(NH):
                for c in range(NC):
                    ty, tx, th, tc = move(y, x, h, c)
                    pairs.append(
                        (((y * NX + x) * NH + h) * NC + c, ((ty * NX + tx) * NH + th) * NC + tc)
                    )
    return pairs


MOVES = {
    "x1": lambda y, x, h, c: (y, x ^ 1, h, c),
    "x3": lambda y, x, h, c: (y, x ^ 3, h, c),
    "y1": lambda y, x, h, c: (y ^ 1, x, h, c),
    "y3": lambda y, x, h, c: (y ^ 3, x, h, c),
    "h": lambda y, x, h, c: (y, x, 1 - h, c),
    "c": lambda y, x, h, c: (y, x, h, 1 - c),
}
FLIPS = {"x1": (0, 1), "x3": (0, 3), "y1": (1, 0), "y3": (3, 0)}
OWN_ORDERS = (("x1", "x3", "y1", "y3"), ("x1", "x3", "y3", "y1"))
OTHER_ORDERS = (("y1", "y3", "x1", "x3"), ("y1", "y3", "x3", "x1"))


def swap(value, kind):
    return lax.ppermute(value, "seq", seq_pairs(MOVES[kind]))


def advance(value, kind):
    return jnp.concatenate([value, swap(value, kind)], axis=0)


def place_kernel(orders, place, *refs):
    pieces = refs[:8]
    out, sem = refs[8:]
    y, x, h, c = (place[i] for i in range(4))
    count, _, part, _ = pieces[0].shape
    for group in range(2):
        half = h if group == 0 else 1 - h
        for last in range(2):
            for side in range(2):
                core = c if side == 0 else 1 - c
                ref = pieces[(group * 2 + last) * 2 + side]
                for k in range(count):
                    flip_y, flip_x = 0, 0
                    for bit, kind in enumerate(orders[group]):
                        if (k + last * count) >> bit & 1:
                            flip_y, flip_x = flip_y ^ FLIPS[kind][0], flip_x ^ FLIPS[kind][1]
                    block = (((y ^ flip_y) * NX + (x ^ flip_x)) * NH + half) * NC + core
                    rows = pl.ds(pl.multiple_of(block * part, 16), part)
                    pltpu.make_async_copy(ref.at[k], out.at[:, rows, :], sem).start()
    pltpu.make_async_copy(out, out, sem).wait()


def place_weights(place, held, received, which):
    held_swapped = [swap(piece, "c") for piece in held]
    received_swapped = [swap(piece, "c") for piece in received]
    pieces = []
    for group in range(2):
        pieces += [held[group], held_swapped[group]]
        pieces += [received[group], received_swapped[group]]
    part, cols = pieces[0].shape[2:]
    total = NY * NX * NH * NC * part
    return pl.pallas_call(
        functools.partial(place_kernel, (OWN_ORDERS[which], OTHER_ORDERS[which])),
        out_shape=jax.ShapeDtypeStruct((3, total, cols), jnp.bfloat16),
        in_specs=[pl.BlockSpec(memory_space=pltpu.SMEM)]
        + [pl.BlockSpec(memory_space=pltpu.HBM)] * 8,
        out_specs=pl.BlockSpec(memory_space=pltpu.VMEM),
        scratch_shapes=[pltpu.SemaphoreType.DMA],
        compiler_params=pltpu.CompilerParams(vmem_limit_bytes=16 * 1024 * 1024),
        cost_estimate=pl.CostEstimate(
            flops=0, bytes_accessed=4 * 3 * total * cols, transcendentals=0
        ),
    )(place, *[pltpu.with_memory_space_constraint(piece, pltpu.HBM) for piece in pieces])


def send_z(value, pairs):
    return lax.ppermute(value, "fsdp", pairs)


def advance_both(pair, which, step):
    return [
        advance(value, orders[which][step])
        for value, orders in zip(pair, (OWN_ORDERS, OTHER_ORDERS))
    ]


def finish_both(pair, which):
    return [
        swap(value, orders[which][3]) for value, orders in zip(pair, (OWN_ORDERS, OTHER_ORDERS))
    ]


def gather_all(tokens, own_strided, own_local):
    split = own_strided.shape[2]
    own = jnp.concatenate([own_strided, own_local], axis=2)[None]
    other = swap(own, "h")
    tokens, other = lax.optimization_barrier((tokens, other))
    near = send_z(tokens, [(0, 1), (1, 0), (2, 3), (3, 2)])
    middle = send_z(tokens, [(1, 2), (2, 1)])
    pair = [own, other]
    for step in range(2):
        pair = advance_both(pair, 0, step)
    strided = advance_both([value[..., :split] for value in pair], 0, 2)
    local = [value[..., split:] for value in pair]
    near, middle, strided, local = lax.optimization_barrier((near, middle, strided, local))
    across = send_z(near, [(1, 2), (2, 1)])
    outward = send_z(middle, [(2, 3), (1, 0)])
    local = advance_both(local, 1, 2)
    received = finish_both(strided, 0)
    across, outward, received, local = lax.optimization_barrier(
        (across, outward, received, local)
    )
    far = send_z(across, [(2, 3), (1, 0)])
    received_local = finish_both(local, 1)
    gathered = (tokens, near, middle, across, outward, far)
    return gathered, (strided, received), (local, received_local)


def shard_slots(z, f):
    if f == z:
        return 0
    if abs(f - z) == 3:
        return 5
    if abs(f - z) == 2:
        return 3 if z in (1, 2) else 4
    return 2 if {f, z} == {1, 2} else 1


def for_shard(z, f, slots, action):
    for slot in slots:
        planes = [plane for plane in range(NZ) if shard_slots(plane, f) == slot]
        if planes:
            here = z == planes[0]
            for plane in planes[1:]:
                here = here | (z == plane)

            @pl.when(here)
            def _(slot=slot):
                action(slot)


def early_kernel(place, *refs):
    tokens, weight = refs[:5], refs[5]
    acc, spare, held, factor, token_sem, weight_sem = refs[6:]
    z = place[4]
    depth = held.shape[2]

    def load(f):
        rows = pl.ds(pl.multiple_of(f * depth, depth), depth)
        return pltpu.make_async_copy(
            weight.at[:, rows, :], factor.at[:, rows, :], weight_sem.at[f]
        )

    for f in range(NZ):
        load(f).start()
        for_shard(
            z,
            f,
            range(5),
            lambda slot, f=f: pltpu.make_async_copy(
                tokens[slot], held.at[f], token_sem.at[f]
            ).start(),
        )
    acc[...] = jnp.zeros_like(acc)

    def step(f, carry):
        load(f).wait()

        @pl.when(jnp.abs(f - z) < NZ - 1)
        def _():
            pltpu.make_async_copy(tokens[0], held.at[f], token_sem.at[f]).wait()
            rows = pl.ds(pl.multiple_of(f * depth, depth), depth)
            for j in range(3):
                acc[j] += jnp.dot(
                    held[f], factor[j, rows, :], preferred_element_type=jnp.float32
                )

        return carry

    lax.fori_loop(0, NZ, step, 0)
    start = pl.multiple_of(jnp.where(z == 0, (NZ - 1) * depth, 0), depth)
    spare[...] = factor[:, pl.ds(start, depth), :]


def late_kernel(place, far, factor, acc, flags, out, held, token_sem):
    z = place[4]
    last = (z == 0) | (z == NZ - 1)
    peers = out.shape[1]
    count = held.shape[0] // peers
    heads = factor.shape[2] // HD

    def store(j, value):
        value = value.astype(out.dtype)
        for head in range(heads):
            for k in range(count):
                out[(j * heads + head) * count + k] = value[
                    k * peers : (k + 1) * peers, head * HD : (head + 1) * HD
                ]

    out[3 * heads * count] = flags[...]

    @pl.when(last)
    def _():
        copy = pltpu.make_async_copy(far, held, token_sem)
        copy.start()
        copy.wait()

        def step(j, carry):
            term = jnp.dot(held[...], factor[j], preferred_element_type=jnp.float32)
            store(j, acc[j] + term)
            return carry

        lax.fori_loop(0, 3, step, 0)

    @pl.when(jnp.logical_not(last))
    def _():
        def step(j, carry):
            store(j, acc[j])
            return carry

        lax.fori_loop(0, 3, step, 0)


def project_early(place, gathered, weight):
    rows, depth = gathered[0].shape
    _, total, cols = weight.shape
    return pl.pallas_call(
        early_kernel,
        out_shape=[
            jax.ShapeDtypeStruct((3, rows, cols), jnp.float32),
            jax.ShapeDtypeStruct((3, depth, cols), jnp.bfloat16),
        ],
        in_specs=[SMEM] + [HBM] * 6,
        out_specs=[VMEM, VMEM],
        scratch_shapes=[
            pltpu.VMEM((NZ, rows, depth), jnp.bfloat16),
            pltpu.VMEM((3, total, cols), jnp.bfloat16),
            pltpu.SemaphoreType.DMA((NZ,)),
            pltpu.SemaphoreType.DMA((NZ,)),
        ],
        compiler_params=pltpu.CompilerParams(vmem_limit_bytes=24 * 1024 * 1024),
        cost_estimate=pl.CostEstimate(
            flops=6 * rows * total * cols,
            bytes_accessed=2 * (rows * total + 3 * total * cols) + 12 * rows * cols,
            transcendentals=0,
        ),
    )(place, *in_hbm(gathered[:5] + (weight,)))


def project_late(place, far, factor, acc, marks):
    rows, depth = far.shape
    cols = factor.shape[2]
    peers = NY * NX * NH * NC
    count = rows // peers
    flags = jnp.transpose(marks.astype(jnp.bfloat16).reshape(count, peers))
    flags = jnp.pad(flags, ((0, 0), (0, HD - count)))
    return pl.pallas_call(
        late_kernel,
        out_shape=jax.ShapeDtypeStruct((3 * cols // HD * count + 1, peers, HD), jnp.bfloat16),
        in_specs=[SMEM, HBM, VMEM, VMEM, VMEM],
        out_specs=VMEM,
        scratch_shapes=[pltpu.VMEM((rows, depth), jnp.bfloat16), pltpu.SemaphoreType.DMA],
        compiler_params=pltpu.CompilerParams(vmem_limit_bytes=16 * 1024 * 1024),
        cost_estimate=pl.CostEstimate(
            flops=6 * rows * depth * cols,
            bytes_accessed=2 * (rows * depth + 3 * depth * cols) + 18 * rows * cols,
            transcendentals=0,
        ),
    )(place, *in_hbm((far,)), factor, acc, flags)


def project_kernel(place, *refs):
    tokens, weight = refs[:6], refs[6]
    out, held, sem = refs[7:]
    depth = held.shape[1] // NZ
    for f in range(NZ):
        cols = held.at[:, pl.ds(f * depth, depth)]
        for_shard(
            place[4],
            f,
            range(6),
            lambda slot, f=f, cols=cols: pltpu.make_async_copy(
                tokens[slot], cols, sem.at[f]
            ).start(),
        )
    for f in range(NZ):
        cols = held.at[:, pl.ds(f * depth, depth)]
        pltpu.make_async_copy(tokens[0], cols, sem.at[f]).wait()

    def step(j, carry):
        out[j] = jnp.dot(
            held[...], weight[j], preferred_element_type=jnp.float32
        ).astype(out.dtype)
        return carry

    lax.fori_loop(0, 3, step, 0)


def project_local(place, gathered, weight):
    rows, depth = gathered[0].shape
    _, total, cols = weight.shape
    return pl.pallas_call(
        project_kernel,
        out_shape=jax.ShapeDtypeStruct((3, rows, cols), jnp.bfloat16),
        in_specs=[SMEM] + [HBM] * 6 + [VMEM],
        out_specs=VMEM,
        scratch_shapes=[
            pltpu.VMEM((rows, total), jnp.bfloat16),
            pltpu.SemaphoreType.DMA((NZ,)),
        ],
        compiler_params=pltpu.CompilerParams(vmem_limit_bytes=20 * 1024 * 1024),
        cost_estimate=pl.CostEstimate(
            flops=6 * rows * total * cols,
            bytes_accessed=2 * (rows * total + 3 * total * cols + 3 * rows * cols),
            transcendentals=0,
        ),
    )(place, *in_hbm(gathered), weight)


def local_attend(qkv, valid_day, reach):
    query, keys, values = qkv[0], qkv[1], qkv[2]
    seconds = query.shape[0]
    query = query.reshape(seconds, -1, HD)
    keys = keys.reshape(seconds, -1, HD)
    values = values.reshape(seconds, -1, HD)
    scores = jnp.einsum(
        "qhc,khc->hqk", query, keys, preferred_element_type=jnp.float32
    ) / math.sqrt(HD)
    position = jnp.arange(seconds)
    causal = position[None, :] <= position[:, None]
    block = position // BLK
    band = block[None, None, :] >= block[None, :, None] - reach[:, None, None]
    seen = (valid_day[None, :] > 0) | (position[None, :] == position[:, None])
    allowed = causal[None] & band & seen[None]
    scores = jnp.where(allowed, scores, -jnp.inf)
    row_max = jnp.max(scores, axis=-1, keepdims=True)
    expo = jnp.exp(scores - row_max)
    probs = (expo / jnp.sum(expo, axis=-1, keepdims=True)).astype(jnp.bfloat16)
    result = jnp.einsum("hqk,khc->qhc", probs, values, preferred_element_type=jnp.float32)
    return result.astype(jnp.bfloat16).reshape(seconds, -1)


def strided_kernel(count, heads, packed, out):
    days = packed.shape[1]
    flags = jnp.transpose(packed[3 * heads * count].astype(jnp.float32))
    span = 2 * days
    row = lax.broadcasted_iota(jnp.int32, (span, span), 0)
    col = lax.broadcasted_iota(jnp.int32, (span, span), 1)
    paired = (row // days) == (col // days)
    earlier = paired & (col < row)
    for second in range(0, count, 2):
        seen = jnp.concatenate(
            [flags[second : second + 1, :], flags[second + 1 : second + 2, :]], axis=1
        )
        allowed = (earlier & (seen > 0)) | (row == col)
        for head in range(heads):
            at = head * count + second
            query, keys, values = (
                packed[pl.ds(at + j * heads * count, 2)].reshape(span, HD) for j in range(3)
            )
            scores = lax.dot_general(
                query, keys, (((1,), (1,)), ((), ())), preferred_element_type=jnp.float32
            ) / math.sqrt(HD)
            scores = jnp.where(allowed, scores, -jnp.inf)
            row_max = jnp.max(scores, axis=1, keepdims=True)
            expo = jnp.exp(scores - row_max)
            probs = (expo / jnp.sum(expo, axis=1, keepdims=True)).astype(jnp.bfloat16)
            result = jnp.dot(probs, values, preferred_element_type=jnp.float32)
            out[pl.ds(at, 2)] = result.astype(jnp.bfloat16).reshape(2, days, HD)


def strided_attend(packed, heads):
    slots, peers, _ = packed.shape
    count = slots // (3 * heads)
    packed = packed.transpose(1, 0, 2)
    packed = lax.all_to_all(packed, "seq", split_axis=0, concat_axis=0, tiled=True)
    packed = packed.transpose(1, 0, 2)
    result = pl.pallas_call(
        functools.partial(strided_kernel, count, heads),
        out_shape=jax.ShapeDtypeStruct((heads * count, peers, HD), jnp.bfloat16),
        in_specs=[VMEM],
        out_specs=VMEM,
        compiler_params=pltpu.CompilerParams(vmem_limit_bytes=8 * 1024 * 1024),
        cost_estimate=pl.CostEstimate(
            flops=8 * heads * count * peers * peers * HD,
            bytes_accessed=2 * 4 * heads * count * peers * HD,
            transcendentals=2 * heads * count * peers * peers,
        ),
    )(packed)
    result = result.transpose(1, 0, 2)
    result = lax.all_to_all(result, "seq", split_axis=0, concat_axis=0, tiled=True)
    result = result.reshape(peers, heads, count, HD).transpose(2, 0, 1, 3)
    return result.reshape(count * peers, heads * HD)


def body(tokens, w_local, w_strided, valid, band_reach):
    seq = lax.axis_index("seq")
    place = jnp.stack(
        [
            seq // (NX * NH * NC),
            seq // (NH * NC) % NX,
            seq // NC % NH,
            seq % NC,
            lax.axis_index("fsdp"),
        ]
    ).astype(jnp.int32)
    own_strided = jnp.transpose(w_strided, (1, 0, 2))
    own_local = jnp.transpose(w_local, (1, 0, 2))
    gathered, strided, local = gather_all(tokens, own_strided, own_local)
    weight_strided = place_weights(place, *strided, 0)
    acc, factor = project_early(place, gathered, weight_strided)
    acc, received = lax.optimization_barrier((acc, local[1]))
    weight_local = place_weights(place, local[0], received, 1)
    packed = project_late(place, gathered[5], factor, acc, valid[0])
    out_strided = strided_attend(packed, w_strided.shape[2] // HD)
    qkv_local = project_local(place, gathered, weight_local)
    out_local = local_attend(qkv_local, valid[0], band_reach)
    return (out_local, out_strided)


def solution(mesh):
    in_specs = (
        P("seq", "fsdp"),
        P("seq", None, "fsdp"),
        P("seq", None, "fsdp"),
        P("seq", None),
        P("fsdp"),
    )
    out_specs = (P("seq", "fsdp"), P("seq", "fsdp"))
    return jax.shard_map(body, mesh=mesh, in_specs=in_specs, out_specs=out_specs, check_vma=False)
```

```python
import functools
import math

import jax
import jax.numpy as jnp
from jax import lax
from jax.experimental import pallas as pl
from jax.experimental.pallas import tpu as pltpu
from jax.sharding import PartitionSpec as P

HD = 128
BLK = 128
NY, NX, NH, NC = 4, 4, 2, 2
NZ = 4


HBM = pl.BlockSpec(memory_space=pltpu.HBM)
VMEM = pl.BlockSpec(memory_space=pltpu.VMEM)
SMEM = pl.BlockSpec(memory_space=pltpu.SMEM)


def in_hbm(values):
    return [pltpu.with_memory_space_constraint(value, pltpu.HBM) for value in values]


def seq_pairs(move):
    pairs = []
    for y in range(NY):
        for x in range(NX):
            for h in range(NH):
                for c in range(NC):
                    ty, tx, th, tc = move(y, x, h, c)
                    pairs.append(
                        (((y * NX + x) * NH + h) * NC + c, ((ty * NX + tx) * NH + th) * NC + tc)
                    )
    return pairs


MOVES = {
    "x1": lambda y, x, h, c: (y, x ^ 1, h, c),
    "x3": lambda y, x, h, c: (y, x ^ 3, h, c),
    "y1": lambda y, x, h, c: (y ^ 1, x, h, c),
    "y3": lambda y, x, h, c: (y ^ 3, x, h, c),
    "h": lambda y, x, h, c: (y, x, 1 - h, c),
    "c": lambda y, x, h, c: (y, x, h, 1 - c),
}
FLIPS = {"x1": (0, 1), "x3": (0, 3), "y1": (1, 0), "y3": (3, 0)}
OWN_ORDERS = (("x1", "x3", "y1", "y3"), ("x1", "x3", "y3", "y1"))
OTHER_ORDERS = (("y1", "y3", "x1", "x3"), ("y1", "y3", "x3", "x1"))


def swap(value, kind):
    return lax.ppermute(value, "seq", seq_pairs(MOVES[kind]))


def advance(value, kind):
    return jnp.concatenate([value, swap(value, kind)], axis=0)


def place_kernel(orders, place, *refs):
    pieces = refs[:8]
    out, sem = refs[8:]
    y, x, h, c = (place[i] for i in range(4))
    count, _, part, _ = pieces[0].shape
    for group in range(2):
        half = h if group == 0 else 1 - h
        for last in range(2):
            for side in range(2):
                core = c if side == 0 else 1 - c
                ref = pieces[(group * 2 + last) * 2 + side]
                for k in range(count):
                    flip_y, flip_x = 0, 0
                    for bit, kind in enumerate(orders[group]):
                        if (k + last * count) >> bit & 1:
                            flip_y, flip_x = flip_y ^ FLIPS[kind][0], flip_x ^ FLIPS[kind][1]
                    block = (((y ^ flip_y) * NX + (x ^ flip_x)) * NH + half) * NC + core
                    rows = pl.ds(pl.multiple_of(block * part, 16), part)
                    pltpu.make_async_copy(ref.at[k], out.at[:, rows, :], sem).start()
    pltpu.make_async_copy(out, out, sem).wait()


def place_weights(place, held, received, which):
    held_swapped = [swap(piece, "c") for piece in held]
    received_swapped = [swap(piece, "c") for piece in received]
    pieces = []
    for group in range(2):
        pieces += [held[group], held_swapped[group]]
        pieces += [received[group], received_swapped[group]]
    part, cols = pieces[0].shape[2:]
    total = NY * NX * NH * NC * part
    return pl.pallas_call(
        functools.partial(place_kernel, (OWN_ORDERS[which], OTHER_ORDERS[which])),
        out_shape=jax.ShapeDtypeStruct((3, total, cols), jnp.bfloat16),
        in_specs=[pl.BlockSpec(memory_space=pltpu.SMEM)]
        + [pl.BlockSpec(memory_space=pltpu.HBM)] * 8,
        out_specs=pl.BlockSpec(memory_space=pltpu.VMEM),
        scratch_shapes=[pltpu.SemaphoreType.DMA],
        compiler_params=pltpu.CompilerParams(vmem_limit_bytes=16 * 1024 * 1024),
        cost_estimate=pl.CostEstimate(
            flops=0, bytes_accessed=4 * 3 * total * cols, transcendentals=0
        ),
    )(place, *[pltpu.with_memory_space_constraint(piece, pltpu.HBM) for piece in pieces])


def send_z(value, pairs):
    return lax.ppermute(value, "fsdp", pairs)


def advance_both(pair, which, step):
    return [
        advance(value, orders[which][step])
        for value, orders in zip(pair, (OWN_ORDERS, OTHER_ORDERS))
    ]


def finish_both(pair, which):
    return [
        swap(value, orders[which][3]) for value, orders in zip(pair, (OWN_ORDERS, OTHER_ORDERS))
    ]


def gather_all(tokens, own_strided, own_local):
    split = own_strided.shape[2]
    own = jnp.concatenate([own_strided, own_local], axis=2)[None]
    other = swap(own, "h")
    tokens, other = lax.optimization_barrier((tokens, other))
    near = send_z(tokens, [(0, 1), (1, 0), (2, 3), (3, 2)])
    middle = send_z(tokens, [(1, 2), (2, 1)])
    pair = [own, other]
    for step in range(2):
        pair = advance_both(pair, 0, step)
    strided = advance_both([value[..., :split] for value in pair], 0, 2)
    local = [value[..., split:] for value in pair]
    near, middle, strided, local = lax.optimization_barrier((near, middle, strided, local))
    across = send_z(near, [(1, 2), (2, 1)])
    outward = send_z(middle, [(2, 3), (1, 0)])
    local = advance_both(local, 1, 2)
    received = finish_both(strided, 0)
    across, outward, received, local = lax.optimization_barrier(
        (across, outward, received, local)
    )
    far = send_z(across, [(2, 3), (1, 0)])
    received_local = finish_both(local, 1)
    gathered = (tokens, near, middle, across, outward, far)
    return gathered, (strided, received), (local, received_local)


def shard_slots(z, f):
    if f == z:
        return 0
    if abs(f - z) == 3:
        return 5
    if abs(f - z) == 2:
        return 3 if z in (1, 2) else 4
    return 2 if {f, z} == {1, 2} else 1


def for_shard(z, f, slots, action):
    for slot in slots:
        planes = [plane for plane in range(NZ) if shard_slots(plane, f) == slot]
        if planes:
            here = z == planes[0]
            for plane in planes[1:]:
                here = here | (z == plane)

            @pl.when(here)
            def _(slot=slot):
                action(slot)


def early_kernel(place, *refs):
    tokens, weight = refs[:5], refs[5]
    acc, held, factor, token_sem, weight_sem = refs[6:]
    z = place[4]
    depth = held.shape[2]

    def load(f):
        rows = pl.ds(pl.multiple_of(f * depth, depth), depth)
        return pltpu.make_async_copy(
            weight.at[:, rows, :], factor.at[:, rows, :], weight_sem.at[f]
        )

    for f in range(NZ):
        load(f).start()
        for_shard(
            z,
            f,
            range(5),
            lambda slot, f=f: pltpu.make_async_copy(
                tokens[slot], held.at[f], token_sem.at[f]
            ).start(),
        )
    acc[...] = jnp.zeros_like(acc)

    def step(f, carry):
        load(f).wait()

        @pl.when(jnp.abs(f - z) < NZ - 1)
        def _():
            pltpu.make_async_copy(tokens[0], held.at[f], token_sem.at[f]).wait()
            rows = pl.ds(pl.multiple_of(f * depth, depth), depth)
            for j in range(3):
                acc[j] += jnp.dot(
                    held[f], factor[j, rows, :], preferred_element_type=jnp.float32
                )

        return carry

    lax.fori_loop(0, NZ, step, 0)


def late_kernel(
    place, far, weight, acc, flags, out, held, factor, token_sem, weight_sem
):
    z = place[4]
    depth = held.shape[1]
    start = pl.multiple_of(jnp.where(z == 0, (NZ - 1) * depth, 0), depth)

    def load(j):
        return pltpu.make_async_copy(
            weight.at[j, pl.ds(start, depth), :], factor.at[j], weight_sem.at[j]
        )

    last = (z == 0) | (z == NZ - 1)
    peers = out.shape[1]
    count = held.shape[0] // peers
    heads = factor.shape[2] // HD

    def store(j, value):
        value = value.astype(out.dtype)
        for head in range(heads):
            for k in range(count):
                out[(j * heads + head) * count + k] = value[
                    k * peers : (k + 1) * peers, head * HD : (head + 1) * HD
                ]

    out[3 * heads * count] = flags[...]

    @pl.when(last)
    def _():
        copy = pltpu.make_async_copy(far, held, token_sem)
        copy.start()
        for j in range(3):
            load(j).start()
        copy.wait()

        def step(j, carry):
            load(j).wait()
            term = jnp.dot(held[...], factor[j], preferred_element_type=jnp.float32)
            store(j, acc[j] + term)
            return carry

        lax.fori_loop(0, 3, step, 0)

    @pl.when(jnp.logical_not(last))
    def _():
        def step(j, carry):
            store(j, acc[j])
            return carry

        lax.fori_loop(0, 3, step, 0)


def project_early(place, gathered, weight):
    rows, depth = gathered[0].shape
    _, total, cols = weight.shape
    return pl.pallas_call(
        early_kernel,
        out_shape=jax.ShapeDtypeStruct((3, rows, cols), jnp.float32),
        in_specs=[SMEM] + [HBM] * 6,
        out_specs=VMEM,
        scratch_shapes=[
            pltpu.VMEM((NZ, rows, depth), jnp.bfloat16),
            pltpu.VMEM((3, total, cols), jnp.bfloat16),
            pltpu.SemaphoreType.DMA((NZ,)),
            pltpu.SemaphoreType.DMA((NZ,)),
        ],
        compiler_params=pltpu.CompilerParams(vmem_limit_bytes=24 * 1024 * 1024),
        cost_estimate=pl.CostEstimate(
            flops=6 * rows * total * cols,
            bytes_accessed=2 * (rows * total + 3 * total * cols) + 12 * rows * cols,
            transcendentals=0,
        ),
    )(place, *in_hbm(gathered[:5] + (weight,)))


def project_late(place, far, weight, acc, marks):
    rows, depth = far.shape
    cols = weight.shape[2]
    peers = NY * NX * NH * NC
    count = rows // peers
    flags = jnp.transpose(marks.astype(jnp.bfloat16).reshape(count, peers))
    flags = jnp.pad(flags, ((0, 0), (0, HD - count)))
    return pl.pallas_call(
        late_kernel,
        out_shape=jax.ShapeDtypeStruct((3 * cols // HD * count + 1, peers, HD), jnp.bfloat16),
        in_specs=[SMEM, HBM, HBM, VMEM, VMEM],
        out_specs=VMEM,
        scratch_shapes=[
            pltpu.VMEM((rows, depth), jnp.bfloat16),
            pltpu.VMEM((3, depth, cols), jnp.bfloat16),
            pltpu.SemaphoreType.DMA,
            pltpu.SemaphoreType.DMA((3,)),
        ],
        compiler_params=pltpu.CompilerParams(vmem_limit_bytes=16 * 1024 * 1024),
        cost_estimate=pl.CostEstimate(
            flops=6 * rows * depth * cols,
            bytes_accessed=2 * (rows * depth + 3 * depth * cols) + 18 * rows * cols,
            transcendentals=0,
        ),
    )(place, *in_hbm((far, weight)), acc, flags)


def project_kernel(place, *refs):
    tokens, weight = refs[:6], refs[6]
    out, held, sem = refs[7:]
    depth = held.shape[1] // NZ
    for f in range(NZ):
        cols = held.at[:, pl.ds(f * depth, depth)]
        for_shard(
            place[4],
            f,
            range(6),
            lambda slot, f=f, cols=cols: pltpu.make_async_copy(
                tokens[slot], cols, sem.at[f]
            ).start(),
        )
    for f in range(NZ):
        cols = held.at[:, pl.ds(f * depth, depth)]
        pltpu.make_async_copy(tokens[0], cols, sem.at[f]).wait()

    def step(j, carry):
        out[j] = jnp.dot(
            held[...], weight[j], preferred_element_type=jnp.float32
        ).astype(out.dtype)
        return carry

    lax.fori_loop(0, 3, step, 0)


def project_local(place, gathered, weight):
    rows, depth = gathered[0].shape
    _, total, cols = weight.shape
    return pl.pallas_call(
        project_kernel,
        out_shape=jax.ShapeDtypeStruct((3, rows, cols), jnp.bfloat16),
        in_specs=[SMEM] + [HBM] * 6 + [VMEM],
        out_specs=VMEM,
        scratch_shapes=[
            pltpu.VMEM((rows, total), jnp.bfloat16),
            pltpu.SemaphoreType.DMA((NZ,)),
        ],
        compiler_params=pltpu.CompilerParams(vmem_limit_bytes=20 * 1024 * 1024),
        cost_estimate=pl.CostEstimate(
            flops=6 * rows * total * cols,
            bytes_accessed=2 * (rows * total + 3 * total * cols + 3 * rows * cols),
            transcendentals=0,
        ),
    )(place, *in_hbm(gathered), weight)


def local_attend(qkv, valid_day, reach):
    query, keys, values = qkv[0], qkv[1], qkv[2]
    seconds = query.shape[0]
    query = query.reshape(seconds, -1, HD)
    keys = keys.reshape(seconds, -1, HD)
    values = values.reshape(seconds, -1, HD)
    scores = jnp.einsum(
        "qhc,khc->hqk", query, keys, preferred_element_type=jnp.float32
    ) / math.sqrt(HD)
    position = jnp.arange(seconds)
    causal = position[None, :] <= position[:, None]
    block = position // BLK
    band = block[None, None, :] >= block[None, :, None] - reach[:, None, None]
    seen = (valid_day[None, :] > 0) | (position[None, :] == position[:, None])
    allowed = causal[None] & band & seen[None]
    scores = jnp.where(allowed, scores, -jnp.inf)
    row_max = jnp.max(scores, axis=-1, keepdims=True)
    expo = jnp.exp(scores - row_max)
    probs = (expo / jnp.sum(expo, axis=-1, keepdims=True)).astype(jnp.bfloat16)
    result = jnp.einsum("hqk,khc->qhc", probs, values, preferred_element_type=jnp.float32)
    return result.astype(jnp.bfloat16).reshape(seconds, -1)


def strided_kernel(count, heads, packed, out):
    days = packed.shape[1]
    flags = jnp.transpose(packed[3 * heads * count].astype(jnp.float32))
    span = 2 * days
    row = lax.broadcasted_iota(jnp.int32, (span, span), 0)
    col = lax.broadcasted_iota(jnp.int32, (span, span), 1)
    paired = (row // days) == (col // days)
    earlier = paired & (col < row)
    for second in range(0, count, 2):
        seen = jnp.concatenate(
            [flags[second : second + 1, :], flags[second + 1 : second + 2, :]], axis=1
        )
        allowed = (earlier & (seen > 0)) | (row == col)
        for head in range(heads):
            at = head * count + second
            query, keys, values = (
                packed[pl.ds(at + j * heads * count, 2)].reshape(span, HD) for j in range(3)
            )
            scores = lax.dot_general(
                query, keys, (((1,), (1,)), ((), ())), preferred_element_type=jnp.float32
            ) / math.sqrt(HD)
            scores = jnp.where(allowed, scores, -jnp.inf)
            row_max = jnp.max(scores, axis=1, keepdims=True)
            expo = jnp.exp(scores - row_max)
            probs = (expo / jnp.sum(expo, axis=1, keepdims=True)).astype(jnp.bfloat16)
            result = jnp.dot(probs, values, preferred_element_type=jnp.float32)
            out[pl.ds(at, 2)] = result.astype(jnp.bfloat16).reshape(2, days, HD)


def strided_attend(packed, heads):
    slots, peers, _ = packed.shape
    count = slots // (3 * heads)
    packed = packed.transpose(1, 0, 2)
    packed = lax.all_to_all(packed, "seq", split_axis=0, concat_axis=0, tiled=True)
    packed = packed.transpose(1, 0, 2)
    result = pl.pallas_call(
        functools.partial(strided_kernel, count, heads),
        out_shape=jax.ShapeDtypeStruct((heads * count, peers, HD), jnp.bfloat16),
        in_specs=[VMEM],
        out_specs=VMEM,
        compiler_params=pltpu.CompilerParams(vmem_limit_bytes=8 * 1024 * 1024),
        cost_estimate=pl.CostEstimate(
            flops=8 * heads * count * peers * peers * HD,
            bytes_accessed=2 * 4 * heads * count * peers * HD,
            transcendentals=2 * heads * count * peers * peers,
        ),
    )(packed)
    result = result.transpose(1, 0, 2)
    result = lax.all_to_all(result, "seq", split_axis=0, concat_axis=0, tiled=True)
    result = result.reshape(peers, heads, count, HD).transpose(2, 0, 1, 3)
    return result.reshape(count * peers, heads * HD)


def body(tokens, w_local, w_strided, valid, band_reach):
    seq = lax.axis_index("seq")
    place = jnp.stack(
        [
            seq // (NX * NH * NC),
            seq // (NH * NC) % NX,
            seq // NC % NH,
            seq % NC,
            lax.axis_index("fsdp"),
        ]
    ).astype(jnp.int32)
    own_strided = jnp.transpose(w_strided, (1, 0, 2))
    own_local = jnp.transpose(w_local, (1, 0, 2))
    gathered, strided, local = gather_all(tokens, own_strided, own_local)
    weight_strided = place_weights(place, *strided, 0)
    acc = project_early(place, gathered, weight_strided)
    acc, received = lax.optimization_barrier((acc, local[1]))
    weight_local = place_weights(place, local[0], received, 1)
    packed = project_late(place, gathered[5], weight_strided, acc, valid[0])
    out_strided = strided_attend(packed, w_strided.shape[2] // HD)
    qkv_local = project_local(place, gathered, weight_local)
    out_local = local_attend(qkv_local, valid[0], band_reach)
    return (out_local, out_strided)


def solution(mesh):
    in_specs = (
        P("seq", "fsdp"),
        P("seq", None, "fsdp"),
        P("seq", None, "fsdp"),
        P("seq", None),
        P("fsdp"),
    )
    out_specs = (P("seq", "fsdp"), P("seq", "fsdp"))
    return jax.shard_map(body, mesh=mesh, in_specs=in_specs, out_specs=out_specs, check_vma=False)
```

```python
import functools
import math

import jax
import jax.numpy as jnp
from jax import lax
from jax.experimental import pallas as pl
from jax.experimental.pallas import tpu as pltpu
from jax.sharding import PartitionSpec as P

HD = 128
BLK = 128
NY, NX, NH, NC = 4, 4, 2, 2
NZ = 4


HBM = pl.BlockSpec(memory_space=pltpu.HBM)
VMEM = pl.BlockSpec(memory_space=pltpu.VMEM)
SMEM = pl.BlockSpec(memory_space=pltpu.SMEM)


def in_hbm(values):
    return [pltpu.with_memory_space_constraint(value, pltpu.HBM) for value in values]


def seq_pairs(move):
    pairs = []
    for y in range(NY):
        for x in range(NX):
            for h in range(NH):
                for c in range(NC):
                    ty, tx, th, tc = move(y, x, h, c)
                    pairs.append(
                        (((y * NX + x) * NH + h) * NC + c, ((ty * NX + tx) * NH + th) * NC + tc)
                    )
    return pairs


MOVES = {
    "x1": lambda y, x, h, c: (y, x ^ 1, h, c),
    "x3": lambda y, x, h, c: (y, x ^ 3, h, c),
    "y1": lambda y, x, h, c: (y ^ 1, x, h, c),
    "y3": lambda y, x, h, c: (y ^ 3, x, h, c),
    "h": lambda y, x, h, c: (y, x, 1 - h, c),
    "c": lambda y, x, h, c: (y, x, h, 1 - c),
}
FLIPS = {"x1": (0, 1), "x3": (0, 3), "y1": (1, 0), "y3": (3, 0)}
OWN_ORDERS = (("x1", "x3", "y1", "y3"), ("x1", "x3", "y3", "y1"))
OTHER_ORDERS = (("y1", "y3", "x1", "x3"), ("y1", "y3", "x3", "x1"))


def swap(value, kind):
    return lax.ppermute(value, "seq", seq_pairs(MOVES[kind]))


def advance(value, kind):
    return jnp.concatenate([value, swap(value, kind)], axis=0)


def place_kernel(orders, place, *refs):
    pieces = refs[:8]
    out, sem = refs[8:]
    y, x, h, c = (place[i] for i in range(4))
    count, _, part, _ = pieces[0].shape
    for group in range(2):
        half = h if group == 0 else 1 - h
        for last in range(2):
            for side in range(2):
                core = c if side == 0 else 1 - c
                ref = pieces[(group * 2 + last) * 2 + side]
                for k in range(count):
                    flip_y, flip_x = 0, 0
                    for bit, kind in enumerate(orders[group]):
                        if (k + last * count) >> bit & 1:
                            flip_y, flip_x = flip_y ^ FLIPS[kind][0], flip_x ^ FLIPS[kind][1]
                    block = (((y ^ flip_y) * NX + (x ^ flip_x)) * NH + half) * NC + core
                    rows = pl.ds(pl.multiple_of(block * part, 16), part)
                    pltpu.make_async_copy(ref.at[k], out.at[:, rows, :], sem).start()
    pltpu.make_async_copy(out, out, sem).wait()


def place_weights(place, held, received, which):
    held_swapped = [swap(piece, "c") for piece in held]
    received_swapped = [swap(piece, "c") for piece in received]
    pieces = []
    for group in range(2):
        pieces += [held[group], held_swapped[group]]
        pieces += [received[group], received_swapped[group]]
    part, cols = pieces[0].shape[2:]
    total = NY * NX * NH * NC * part
    return pl.pallas_call(
        functools.partial(place_kernel, (OWN_ORDERS[which], OTHER_ORDERS[which])),
        out_shape=jax.ShapeDtypeStruct((3, total, cols), jnp.bfloat16),
        in_specs=[pl.BlockSpec(memory_space=pltpu.SMEM)]
        + [pl.BlockSpec(memory_space=pltpu.HBM)] * 8,
        out_specs=pl.BlockSpec(memory_space=pltpu.VMEM),
        scratch_shapes=[pltpu.SemaphoreType.DMA],
        compiler_params=pltpu.CompilerParams(vmem_limit_bytes=16 * 1024 * 1024),
        cost_estimate=pl.CostEstimate(
            flops=0, bytes_accessed=total * cols // 16, transcendentals=0
        ),
    )(place, *[pltpu.with_memory_space_constraint(piece, pltpu.HBM) for piece in pieces])


def send_z(value, pairs):
    return lax.ppermute(value, "fsdp", pairs)


def advance_both(pair, which, step):
    return [
        advance(value, orders[which][step])
        for value, orders in zip(pair, (OWN_ORDERS, OTHER_ORDERS))
    ]


def finish_both(pair, which):
    return [
        swap(value, orders[which][3]) for value, orders in zip(pair, (OWN_ORDERS, OTHER_ORDERS))
    ]


def gather_all(tokens, own_strided, own_local):
    split = own_strided.shape[2]
    own = jnp.concatenate([own_strided, own_local], axis=2)[None]
    other = swap(own, "h")
    tokens, other = lax.optimization_barrier((tokens, other))
    near = send_z(tokens, [(0, 1), (1, 0), (2, 3), (3, 2)])
    middle = send_z(tokens, [(1, 2), (2, 1)])
    pair = [own, other]
    for step in range(2):
        pair = advance_both(pair, 0, step)
    strided = advance_both([value[..., :split] for value in pair], 0, 2)
    local = [value[..., split:] for value in pair]
    near, middle, strided, local = lax.optimization_barrier((near, middle, strided, local))
    across = send_z(near, [(1, 2), (2, 1)])
    outward = send_z(middle, [(2, 3), (1, 0)])
    local = advance_both(local, 1, 2)
    received = finish_both(strided, 0)
    across, outward, received, local = lax.optimization_barrier(
        (across, outward, received, local)
    )
    far = send_z(across, [(2, 3), (1, 0)])
    received_local = finish_both(local, 1)
    gathered = (tokens, near, middle, across, outward, far)
    return gathered, (strided, received), (local, received_local)


def shard_slots(z, f):
    if f == z:
        return 0
    if abs(f - z) == 3:
        return 5
    if abs(f - z) == 2:
        return 3 if z in (1, 2) else 4
    return 2 if {f, z} == {1, 2} else 1


def for_shard(z, f, slots, action):
    for slot in slots:
        planes = [plane for plane in range(NZ) if shard_slots(plane, f) == slot]
        if planes:
            here = z == planes[0]
            for plane in planes[1:]:
                here = here | (z == plane)

            @pl.when(here)
            def _(slot=slot):
                action(slot)


def early_kernel(place, *refs):
    tokens, weight = refs[:5], refs[5]
    acc, held, factor, token_sem, weight_sem = refs[6:]
    z = place[4]
    depth = held.shape[2]

    def load(f):
        rows = pl.ds(pl.multiple_of(f * depth, depth), depth)
        return pltpu.make_async_copy(
            weight.at[:, rows, :], factor.at[:, rows, :], weight_sem.at[f]
        )

    for f in range(NZ):
        load(f).start()
        for_shard(
            z,
            f,
            range(5),
            lambda slot, f=f: pltpu.make_async_copy(
                tokens[slot], held.at[f], token_sem.at[f]
            ).start(),
        )
    acc[...] = jnp.zeros_like(acc)

    def step(f, carry):
        load(f).wait()

        @pl.when(jnp.abs(f - z) < NZ - 1)
        def _():
            pltpu.make_async_copy(tokens[0], held.at[f], token_sem.at[f]).wait()
            rows = pl.ds(pl.multiple_of(f * depth, depth), depth)
            for j in range(3):
                acc[j] += jnp.dot(
                    held[f], factor[j, rows, :], preferred_element_type=jnp.float32
                )

        return carry

    lax.fori_loop(0, NZ, step, 0)


def late_kernel(
    place, far, weight, acc, flags, out, held, factor, token_sem, weight_sem
):
    z = place[4]
    depth = held.shape[1]
    start = pl.multiple_of(jnp.where(z == 0, (NZ - 1) * depth, 0), depth)

    def load(j):
        return pltpu.make_async_copy(
            weight.at[j, pl.ds(start, depth), :], factor.at[j], weight_sem.at[j]
        )

    last = (z == 0) | (z == NZ - 1)
    peers = out.shape[1]
    count = held.shape[0] // peers
    heads = factor.shape[2] // HD

    def store(j, value):
        value = value.astype(out.dtype)
        for head in range(heads):
            for k in range(count):
                out[(j * heads + head) * count + k] = value[
                    k * peers : (k + 1) * peers, head * HD : (head + 1) * HD
                ]

    out[3 * heads * count] = flags[...]

    @pl.when(last)
    def _():
        copy = pltpu.make_async_copy(far, held, token_sem)
        copy.start()
        for j in range(3):
            load(j).start()
        copy.wait()

        def step(j, carry):
            load(j).wait()
            term = jnp.dot(held[...], factor[j], preferred_element_type=jnp.float32)
            store(j, acc[j] + term)
            return carry

        lax.fori_loop(0, 3, step, 0)

    @pl.when(jnp.logical_not(last))
    def _():
        def step(j, carry):
            store(j, acc[j])
            return carry

        lax.fori_loop(0, 3, step, 0)


def project_early(place, gathered, weight):
    rows, depth = gathered[0].shape
    _, total, cols = weight.shape
    return pl.pallas_call(
        early_kernel,
        out_shape=jax.ShapeDtypeStruct((3, rows, cols), jnp.float32),
        in_specs=[SMEM] + [HBM] * 6,
        out_specs=VMEM,
        scratch_shapes=[
            pltpu.VMEM((NZ, rows, depth), jnp.bfloat16),
            pltpu.VMEM((3, total, cols), jnp.bfloat16),
            pltpu.SemaphoreType.DMA((NZ,)),
            pltpu.SemaphoreType.DMA((NZ,)),
        ],
        compiler_params=pltpu.CompilerParams(vmem_limit_bytes=24 * 1024 * 1024),
        cost_estimate=pl.CostEstimate(
            flops=rows * total * cols // 16,
            bytes_accessed=(rows * total + 3 * total * cols) // 16,
            transcendentals=0,
        ),
    )(place, *in_hbm(gathered[:5] + (weight,)))


def project_late(place, far, weight, acc, marks):
    rows, depth = far.shape
    cols = weight.shape[2]
    peers = NY * NX * NH * NC
    count = rows // peers
    flags = jnp.transpose(marks.astype(jnp.bfloat16).reshape(count, peers))
    flags = jnp.pad(flags, ((0, 0), (0, HD - count)))
    return pl.pallas_call(
        late_kernel,
        out_shape=jax.ShapeDtypeStruct((3 * cols // HD * count + 1, peers, HD), jnp.bfloat16),
        in_specs=[SMEM, HBM, HBM, VMEM, VMEM],
        out_specs=VMEM,
        scratch_shapes=[
            pltpu.VMEM((rows, depth), jnp.bfloat16),
            pltpu.VMEM((3, depth, cols), jnp.bfloat16),
            pltpu.SemaphoreType.DMA,
            pltpu.SemaphoreType.DMA((3,)),
        ],
        compiler_params=pltpu.CompilerParams(vmem_limit_bytes=16 * 1024 * 1024),
        cost_estimate=pl.CostEstimate(
            flops=6 * rows * depth * cols,
            bytes_accessed=2 * (rows * depth + 3 * depth * cols) + 18 * rows * cols,
            transcendentals=0,
        ),
    )(place, *in_hbm((far, weight)), acc, flags)


def project_kernel(place, *refs):
    tokens, weight = refs[:6], refs[6]
    out, held, sem = refs[7:]
    depth = held.shape[1] // NZ
    for f in range(NZ):
        cols = held.at[:, pl.ds(f * depth, depth)]
        for_shard(
            place[4],
            f,
            range(6),
            lambda slot, f=f, cols=cols: pltpu.make_async_copy(
                tokens[slot], cols, sem.at[f]
            ).start(),
        )
    for f in range(NZ):
        cols = held.at[:, pl.ds(f * depth, depth)]
        pltpu.make_async_copy(tokens[0], cols, sem.at[f]).wait()

    def step(j, carry):
        out[j] = jnp.dot(
            held[...], weight[j], preferred_element_type=jnp.float32
        ).astype(out.dtype)
        return carry

    lax.fori_loop(0, 3, step, 0)


def project_local(place, gathered, weight):
    rows, depth = gathered[0].shape
    _, total, cols = weight.shape
    return pl.pallas_call(
        project_kernel,
        out_shape=jax.ShapeDtypeStruct((3, rows, cols), jnp.bfloat16),
        in_specs=[SMEM] + [HBM] * 6 + [VMEM],
        out_specs=VMEM,
        scratch_shapes=[
            pltpu.VMEM((rows, total), jnp.bfloat16),
            pltpu.SemaphoreType.DMA((NZ,)),
        ],
        compiler_params=pltpu.CompilerParams(vmem_limit_bytes=20 * 1024 * 1024),
        cost_estimate=pl.CostEstimate(
            flops=6 * rows * total * cols,
            bytes_accessed=2 * (rows * total + 3 * total * cols + 3 * rows * cols),
            transcendentals=0,
        ),
    )(place, *in_hbm(gathered), weight)


def local_attend(qkv, valid_day, reach):
    query, keys, values = qkv[0], qkv[1], qkv[2]
    seconds = query.shape[0]
    query = query.reshape(seconds, -1, HD)
    keys = keys.reshape(seconds, -1, HD)
    values = values.reshape(seconds, -1, HD)
    scores = jnp.einsum(
        "qhc,khc->hqk", query, keys, preferred_element_type=jnp.float32
    ) / math.sqrt(HD)
    position = jnp.arange(seconds)
    causal = position[None, :] <= position[:, None]
    block = position // BLK
    band = block[None, None, :] >= block[None, :, None] - reach[:, None, None]
    seen = (valid_day[None, :] > 0) | (position[None, :] == position[:, None])
    allowed = causal[None] & band & seen[None]
    scores = jnp.where(allowed, scores, -jnp.inf)
    row_max = jnp.max(scores, axis=-1, keepdims=True)
    expo = jnp.exp(scores - row_max)
    probs = (expo / jnp.sum(expo, axis=-1, keepdims=True)).astype(jnp.bfloat16)
    result = jnp.einsum("hqk,khc->qhc", probs, values, preferred_element_type=jnp.float32)
    return result.astype(jnp.bfloat16).reshape(seconds, -1)


def strided_kernel(count, heads, packed, out):
    days = packed.shape[1]
    flags = jnp.transpose(packed[3 * heads * count].astype(jnp.float32))
    span = 2 * days
    row = lax.broadcasted_iota(jnp.int32, (span, span), 0)
    col = lax.broadcasted_iota(jnp.int32, (span, span), 1)
    paired = (row // days) == (col // days)
    earlier = paired & (col < row)
    for second in range(0, count, 2):
        seen = jnp.concatenate(
            [flags[second : second + 1, :], flags[second + 1 : second + 2, :]], axis=1
        )
        allowed = (earlier & (seen > 0)) | (row == col)
        for head in range(heads):
            at = head * count + second
            query, keys, values = (
                packed[pl.ds(at + j * heads * count, 2)].reshape(span, HD) for j in range(3)
            )
            scores = lax.dot_general(
                query, keys, (((1,), (1,)), ((), ())), preferred_element_type=jnp.float32
            ) / math.sqrt(HD)
            scores = jnp.where(allowed, scores, -jnp.inf)
            row_max = jnp.max(scores, axis=1, keepdims=True)
            expo = jnp.exp(scores - row_max)
            probs = (expo / jnp.sum(expo, axis=1, keepdims=True)).astype(jnp.bfloat16)
            result = jnp.dot(probs, values, preferred_element_type=jnp.float32)
            out[pl.ds(at, 2)] = result.astype(jnp.bfloat16).reshape(2, days, HD)


def strided_attend(packed, heads):
    slots, peers, _ = packed.shape
    count = slots // (3 * heads)
    packed = packed.transpose(1, 0, 2)
    packed = lax.all_to_all(packed, "seq", split_axis=0, concat_axis=0, tiled=True)
    packed = packed.transpose(1, 0, 2)
    result = pl.pallas_call(
        functools.partial(strided_kernel, count, heads),
        out_shape=jax.ShapeDtypeStruct((heads * count, peers, HD), jnp.bfloat16),
        in_specs=[VMEM],
        out_specs=VMEM,
        compiler_params=pltpu.CompilerParams(vmem_limit_bytes=8 * 1024 * 1024),
        cost_estimate=pl.CostEstimate(
            flops=8 * heads * count * peers * peers * HD,
            bytes_accessed=2 * 4 * heads * count * peers * HD,
            transcendentals=2 * heads * count * peers * peers,
        ),
    )(packed)
    result = result.transpose(1, 0, 2)
    result = lax.all_to_all(result, "seq", split_axis=0, concat_axis=0, tiled=True)
    result = result.reshape(peers, heads, count, HD).transpose(2, 0, 1, 3)
    return result.reshape(count * peers, heads * HD)


def body(tokens, w_local, w_strided, valid, band_reach):
    seq = lax.axis_index("seq")
    place = jnp.stack(
        [
            seq // (NX * NH * NC),
            seq // (NH * NC) % NX,
            seq // NC % NH,
            seq % NC,
            lax.axis_index("fsdp"),
        ]
    ).astype(jnp.int32)
    own_strided = jnp.transpose(w_strided, (1, 0, 2))
    own_local = jnp.transpose(w_local, (1, 0, 2))
    gathered, strided, local = gather_all(tokens, own_strided, own_local)
    weight_strided = place_weights(place, *strided, 0)
    acc = project_early(place, gathered, weight_strided)
    acc, received = lax.optimization_barrier((acc, local[1]))
    weight_local = place_weights(place, local[0], received, 1)
    packed = project_late(place, gathered[5], weight_strided, acc, valid[0])
    out_strided = strided_attend(packed, w_strided.shape[2] // HD)
    qkv_local = project_local(place, gathered, weight_local)
    out_local = local_attend(qkv_local, valid[0], band_reach)
    return (out_local, out_strided)


def solution(mesh):
    in_specs = (
        P("seq", "fsdp"),
        P("seq", None, "fsdp"),
        P("seq", None, "fsdp"),
        P("seq", None),
        P("fsdp"),
    )
    out_specs = (P("seq", "fsdp"), P("seq", "fsdp"))
    return jax.shard_map(body, mesh=mesh, in_specs=in_specs, out_specs=out_specs, check_vma=False)
```
